128 devices in a mesh: pairs: 32 (over x, y, core), fit: 4 (over z).
Axes of the slice: x: 4, y: 4, z: 4, core: 2. Of those that a mesh axis runs over, the one named last changes fastest.
Arguments:
- b_first: bfloat16 [256, 160, 3072], P('pairs', None, 'fit'), may hold values from -0.109375 to 0.109375
- b_second: bfloat16 [256, 160, 3072], P('pairs', None, 'fit'), may hold values from -6 to 6
- start_amplitudes: float32 [256, 160, 160], P('pairs'), may hold values from -1.8 to 1.8
- margins: bfloat16 [256, 96, 160, 160], P('pairs', 'fit'), may hold values from -0.5 to 0.5
- fock_terms: float32 [256, 96], P('pairs', 'fit'), may hold values from -0.2 to 0.2
- partners: int32 [256, 96], P('pairs', 'fit'), may hold values from 0 to 255, as said below
- pno_energy: float32 [256, 160], P('pairs'), may hold values from 0.3 to 1.5
- occ_energy: float32 [4000], replicated, may hold values from -1 to -0.2
- pair_list: int32 [256, 2], P('pairs'), may hold values from 0 to 3999
- pno_count: int32 [256], P('pairs'), may hold values from 64 to 160, as said below
Outputs:
- amplitudes: float32 [256, 160, 160], P('pairs')
- residual: float32 [256, 160, 160], P('pairs')
The draws below stay inside these ranges and needn't reach their ends.
Inputs may be any that keep to these rules, and one draw needn't show every extreme that they name: `pno_count`: each pair's PNO count is one of 64, 128 and 160. `partners`: pairs owner * 8 to owner * 8 + 7 belong to one owner. In the block of one device (its 8 rows and the columns of its index along fit), each owner's pairs appear at most 12 times, and one owner's pairs appear exactly 12 times in every block.
All inputs are finite; a program needn't handle non-finite values.
Results may differ from the reference program's by a relative error of at most 0.0041.
Values may be sent and summed in bfloat16 or wider, within the bound.
No kernel may reach another device: no remote copies, remote signals or barrier semaphores. Data moves between devices by JAX's collectives and lax.ppermute only.
A program may use at most 192 MiB of HBM per device.

```python
from functools import partial
import jax
import jax.numpy as jnp
from jax import lax

NPNO = 160
FIT = 3072
NOCC = 4000
PARTNERS = 96
ITERS = 2
PAIR_DEV = 8
PAIRS = 256
N_PAIRS = 32
N_FIT = 4


def block_partners(common_owner, key):
    order_key, pick_key, local_key = jax.random.split(key, 3)
    request_count = PAIR_DEV * PARTNERS // N_FIT
    capacity = 2 * request_count // N_PAIRS
    slot_owner = jnp.arange(N_PAIRS * capacity, dtype=jnp.int32) // capacity
    rotated = (slot_owner + common_owner) % N_PAIRS
    remaining = jax.random.permutation(order_key, rotated[capacity:])
    chosen = jnp.concatenate([rotated[:capacity], remaining])[:request_count]
    chosen = jax.random.permutation(pick_key, chosen)
    local_index = jax.random.randint(local_key, (request_count,), 0, PAIR_DEV)
    return (chosen * PAIR_DEV + local_index).reshape(PAIR_DEV, PARTNERS // N_FIT)


def draw_partners(key, part):
    common_owner = jax.random.randint(jax.random.fold_in(key, 7), (), 0, N_PAIRS)
    block_keys = jax.random.split(jax.random.fold_in(key, 11), N_PAIRS * N_FIT)
    blocks = jax.vmap(lambda single: block_partners(common_owner, single))(block_keys)
    blocks = blocks.reshape(N_PAIRS, N_FIT, PAIR_DEV, PARTNERS // N_FIT)
    return jnp.transpose(blocks, (0, 2, 1, 3)).reshape(PAIRS, PARTNERS).astype(jnp.int32)


def draw_pno_count(key, part):
    level_index = jax.random.randint(jax.random.fold_in(key, 3), (PAIRS,), 0, 3)
    level_table = jnp.array([NPNO * 2 // 5, NPNO * 4 // 5, NPNO], dtype=jnp.int32)
    return level_table[level_index]


def touch_ends(result, own_key, least, largest):
    index_at = [jax.random.randint(jax.random.fold_in(own_key, axis), (), 0, length) for axis, length in enumerate(result.shape)]
    longest = result.shape.index(max(result.shape))
    next_to = index_at[:longest] + [(index_at[longest] + 1) % result.shape[longest]] + index_at[longest + 1:]
    return result.at[tuple(index_at)].set(least).at[tuple(next_to)].set(largest)


def level_of(rng, extent, shards, least, largest):
    factor_of = 1.0
    for position, parts in shards:
        draws = jax.random.uniform(jax.random.fold_in(jax.random.fold_in(rng, 6), position), (parts,), jnp.float32, least / len(shards), largest / len(shards))
        factor_of = factor_of * jnp.repeat(jnp.exp(draws), extent[position] // parts).reshape((-1,) + (1,) * (len(extent) - 1 - position))
    return factor_of


def bell_draw(key, shape, scale, reach, cuts=(), held_as=jnp.bfloat16):
    loudness = level_of(key, shape, cuts, -0.22, 0.18) if cuts else 1.0
    entries = jax.random.normal(key, shape, jnp.float32) * scale * loudness
    return jnp.minimum(jnp.maximum(entries, -reach), reach).astype(held_as)


def setup_inputs(seed: int = 0) -> dict:
    splits = jax.random.split(jax.random.key(seed), 11)
    return {
        "b_first": bell_draw(splits[0], (PAIRS, NPNO, FIT), FIT ** -0.5, 0.109375, ((0, 32), (2, 4))),
        "b_second": bell_draw(splits[1], (PAIRS, NPNO, FIT), 1.0, 6.0, ((0, 32), (2, 4))),
        "start_amplitudes": bell_draw(splits[2], (PAIRS, NPNO, NPNO), 0.3, 1.8, ((0, 32),), jnp.float32),
        "margins": bell_draw(splits[3], (PAIRS, PARTNERS, NPNO, NPNO), NPNO ** -0.5, 0.5, ((0, 32), (1, 4))),
        "fock_terms": jnp.clip(jax.random.uniform(splits[4], (PAIRS, PARTNERS), jnp.float32, -0.2, 0.2) * level_of(splits[4], (PAIRS, PARTNERS), ((0, 32), (1, 4)), -0.4, 0.0), -0.2, 0.2),
        "partners": draw_partners(jax.random.fold_in(splits[10], 71), 0),
        "pno_energy": jnp.clip(0.3 + 1.2 * jax.random.uniform(splits[6], (PAIRS, NPNO), jnp.float32) ** level_of(splits[6], (PAIRS, NPNO), ((0, 32),), -0.2, 0.2), 0.3, 1.5),
        "occ_energy": jnp.clip(jax.random.uniform(splits[7], (NOCC,), jnp.float32, -1.0, -0.2), -1.0, -0.2),
        "pair_list": touch_ends(jax.random.randint(splits[8], (PAIRS, 2), 0, NOCC), jax.random.fold_in(splits[8], 1), 0, NOCC - 1).astype(jnp.int32),
        "pno_count": draw_pno_count(jax.random.fold_in(splits[10], 71), 0),
    }


def pair_coupling(rounded, pieces):
    margin_rows, fock_row, partner_row = pieces
    fetched = rounded[partner_row].astype(jnp.float32)
    margin_block = margin_rows.astype(jnp.float32)
    left_product = jnp.einsum("pac,pcd->pad", margin_block, fetched, precision=lax.Precision.HIGHEST)
    left_product = lax.optimization_barrier(left_product.astype(jnp.bfloat16)).astype(jnp.float32)
    right_product = jnp.einsum("pad,pbd->pab", left_product, margin_block, precision=lax.Precision.HIGHEST)
    return jnp.sum(fock_row[:, None, None] * right_product, axis=0)


def pair_integrals(pieces):
    return jnp.dot(pieces[0], pieces[1].T, preferred_element_type=jnp.float32)


def reference(b_first, b_second, start_amplitudes, margins, fock_terms, partners, pno_energy, occ_energy, pair_list, pno_count):
    levels = jnp.arange(NPNO, dtype=jnp.int32)
    keep_rows = (levels[None, :] < pno_count[:, None]).astype(jnp.float32)
    pair_mask = keep_rows[:, :, None] * keep_rows[:, None, :]
    occ_pair = occ_energy[pair_list[:, 0]] + occ_energy[pair_list[:, 1]]
    denominator = pno_energy[:, :, None] + pno_energy[:, None, :] - occ_pair[:, None, None]
    integrals = lax.map(pair_integrals, (b_first, b_second))
    amplitudes = pair_mask * start_amplitudes
    residual = jnp.zeros_like(amplitudes)
    for iteration in range(ITERS):
        rounded = amplitudes.astype(jnp.bfloat16)
        coupling = lax.map(partial(pair_coupling, rounded), (margins, fock_terms, partners))
        residual = pair_mask * (integrals - coupling + denominator * amplitudes)
        amplitudes = amplitudes - residual / denominator
    return amplitudes, residual
```

```python
import functools
import jax
import jax.numpy as jnp
from jax import lax
from jax.experimental import pallas as pl
from jax.experimental.pallas import tpu as pltpu
from jax.sharding import PartitionSpec as P

NPNO = 160
MAIN = 128
TAIL = NPNO - MAIN
PAIR_DEV = 8
COUPLES = 4
NFIT = 4
PER_PAIR = 24
FIT_DEV = 768
CROWS = 400
SHARD = COUPLES * CROWS
ROW4 = 4 * SHARD
ALL = ("pairs", "fit")
F32 = jnp.float32
BF16 = jnp.bfloat16
VMEM = pltpu.VMEM
SMEM = pltpu.SMEM


def lin(x, y, c, z):
    return ((x % 4) * 4 + (y % 4)) * 8 + c * 4 + (z % 4)


def device_list():
    return [(x, y, c, z) for x in range(4) for y in range(4) for c in range(2) for z in range(4)]


def ring(step, first):
    pairs = []
    for x, y, c, z in device_list():
        along_x = (c == 0) == first
        dx, dy = (step, 0) if along_x else (0, step)
        pairs.append((lin(x, y, c, z), lin(x + dx, y + dy, c, z)))
    return pairs


SWAP = [(lin(x, y, c, z), lin(x, y, 1 - c, z)) for x, y, c, z in device_list()]


def fit_shift(step):
    return [(lin(x, y, c, z), lin(x, y, c, z + step)) for x, y, c, z in device_list()]


def send(value, perm):
    return lax.ppermute(value, ALL, perm)


def gather_blocks(shard):
    half = SHARD // 2
    near_p = send(shard, ring(1, True))
    near_m = send(shard, ring(-1, True))
    far_p = send(near_p[:half], ring(1, True))
    far_m = send(near_m[half:], ring(-1, True))
    row = jnp.concatenate([shard, near_p, near_m, far_p, far_m])
    half = ROW4 // 2
    next_p = send(row, ring(1, False))
    next_m = send(row, ring(-1, False))
    row_x = send(row, SWAP)
    last_p = send(next_p[:half], ring(1, False))
    last_m = send(next_m[half:], ring(-1, False))
    next_p_x = send(next_p, SWAP)
    next_m_x = send(next_m, SWAP)
    last_p_x = send(last_p, SWAP)
    last_m_x = send(last_m, SWAP)
    return (row, next_p, next_m, last_p, last_m, row_x, next_p_x, next_m_x, last_p_x, last_m_x)


BLOCK_ROWS = (ROW4, ROW4, ROW4, ROW4 // 2, ROW4 // 2) * 2
BLOCK_AT = tuple(sum(BLOCK_ROWS[:i]) for i in range(len(BLOCK_ROWS)))
TOTAL_ROWS = sum(BLOCK_ROWS)


def locate(partners, me, z):
    x, y, c = me // 8, (me // 2) % 4, me % 2
    owner, local = partners // 8, partners % 8
    ox, oy, oc = owner // 8, (owner // 2) % 4, owner % 2
    dx, dy = (ox - x) & 3, (oy - y) & 3
    da = jnp.where(oc == 0, dx, dy)
    db = jnp.where(oc == 0, dy, dx)
    slot_a = jnp.where(da == 0, 0, jnp.where(da == 3, 1, jnp.where(da == 1, 2, 3)))
    slot_b = jnp.where(db == 0, 0, jnp.where(db == 3, 1, jnp.where(db == 1, 2, 3)))
    couple = (local // 2 - z) & 3
    base = ((oc ^ c) * 4 + slot_b) * ROW4 + slot_a * SHARD + couple * CROWS
    return base * 2 + (local & 1)


def pack_couple(v0, v1):
    t = jnp.concatenate([v0[:, MAIN:], v1[:, MAIN:]], axis=1)
    tail = jnp.concatenate([t[:80], t[80:]], axis=1)
    return v0[:, :MAIN], v1[:, :MAIN], tail


def store_couple(ref, at, v0, v1):
    m0, m1, tail = pack_couple(v0, v1)
    ref[pl.ds(at, 160), :] = m0.astype(ref.dtype)
    ref[pl.ds(at + 160, 160), :] = m1.astype(ref.dtype)
    ref[pl.ds(at + 320, 80), :] = tail.astype(ref.dtype)


def load_couple(ref, at):
    m0 = ref[pl.ds(at, 160), :].astype(F32)
    m1 = ref[pl.ds(at + 160, 160), :].astype(F32)
    tail = ref[pl.ds(at + 320, 80), :].astype(F32)
    t = jnp.concatenate([tail[:, :64], tail[:, 64:]], axis=0)
    return (
        jnp.concatenate([m0, t[:, :TAIL]], axis=1),
        jnp.concatenate([m1, t[:, TAIL:]], axis=1),
    )


def mask_of(count):
    rows = lax.broadcasted_iota(jnp.int32, (NPNO, NPNO), 0)
    cols = lax.broadcasted_iota(jnp.int32, (NPNO, NPNO), 1)
    return (rows < count) & (cols < count)


def pack_kernel(z_ref, count_ref, start_ref, out_ref):
    z = z_ref[0]
    for k in range(COUPLES):
        slot = (k - z + 4) % 4
        v = [jnp.where(mask_of(count_ref[2 * k + i]), start_ref[2 * k + i], 0.0) for i in range(2)]
        store_couple(out_ref, pl.multiple_of(slot * CROWS, 16), *v)


def pack_start(z1, count, start):
    return pl.pallas_call(
        pack_kernel,
        out_shape=jax.ShapeDtypeStruct((SHARD, MAIN), BF16),
        in_specs=[pl.BlockSpec(memory_space=SMEM)] * 2 + [pl.BlockSpec(memory_space=VMEM)],
        out_specs=pl.BlockSpec(memory_space=VMEM),
    )(z1, count, start)


def fixed_kernel(z_ref, first_ref, second_ref, i0, i1, i2, i3):
    k = pl.program_id(0)
    v = [
        lax.dot_general(
            first_ref[i], second_ref[i], (((1,), (1,)), ((), ())), preferred_element_type=F32
        )
        for i in range(2)
    ]
    slot = (k - z_ref[0] + 4) % 4
    for s, ref in enumerate((i0, i1, i2, i3)):

        @pl.when(slot == s)
        def _():
            store_couple(ref, 0, *v)


def integral_parts(z1, first, second):
    spec = pl.BlockSpec((2, NPNO, FIT_DEV), lambda k, z: (k, 0, 0))
    out = pl.BlockSpec((CROWS, MAIN), lambda k, z: (0, 0))
    return pl.pallas_call(
        fixed_kernel,
        out_shape=[jax.ShapeDtypeStruct((CROWS, MAIN), F32)] * 4,
        grid_spec=pltpu.PrefetchScalarGridSpec(
            num_scalar_prefetch=1, grid=(COUPLES,), in_specs=[spec, spec], out_specs=[out] * 4
        ),
        cost_estimate=pl.CostEstimate(
            flops=2 * 8 * 160 * 160 * 768, bytes_accessed=4 * 8 * 160 * 768, transcendentals=0
        ),
    )(z1, first, second)


def coupling_kernel(z_ref, where_ref, fock_ref, margin_ref, *rest):
    blocks = rest[:10]
    outs = rest[10:14]
    held, acc, sems = rest[14:]
    r = pl.program_id(0)
    step = pl.program_id(1)
    n = margin_ref.shape[1]

    @pl.when((r == 0) & (step == 0))
    def _():
        copies = [
            pltpu.make_async_copy(b, held.at[pl.ds(at, rows), :], sems.at[i])
            for i, (b, at, rows) in enumerate(zip(blocks, BLOCK_AT, BLOCK_ROWS))
        ]
        for copy in copies:
            copy.start()
        for copy in copies:
            copy.wait()

    total = None
    for j in range(n):
        item = r * PER_PAIR + step * n + j
        code = where_ref[item]
        odd = code & 1
        base = pl.multiple_of(code >> 1, 16)
        margin = margin_ref[0, j]
        main = held[pl.ds(pl.multiple_of(base + odd * 160, 16), 160), :]
        tail = held[pl.ds(base + 320, 80), :]
        wrapped = jnp.concatenate([tail[:, 64:], tail[:, :64]], axis=1)
        right = jnp.concatenate([main, jnp.concatenate([tail, wrapped], axis=0)], axis=1)
        left = jnp.dot(margin, right, preferred_element_type=F32)
        left_tail = pltpu.roll(left[:, MAIN:], odd * 96, axis=1)
        left = jnp.concatenate([left[:, :MAIN], left_tail[:, :TAIL]], axis=1).astype(BF16)
        term = lax.dot_general(
            left, margin, (((1,), (1,)), ((), ())), preferred_element_type=F32
        )
        term = fock_ref[item] * term
        total = term if total is None else total + term

    @pl.when(step == 0)
    def _():
        acc[r] = total

    @pl.when(step > 0)
    def _():
        acc[r] += total

    @pl.when((r == pl.num_programs(0) - 1) & (step == pl.num_programs(1) - 1))
    def _():
        z = z_ref[0]
        for s in range(NFIT):
            k = (z + s) % 4
            store_couple(outs[s], 0, acc[2 * k], acc[2 * k + 1])


def coupling_parts(z1, where, fock, margins, blocks):
    n = 8
    any_spec = pl.BlockSpec(memory_space=pl.ANY)
    out = pl.BlockSpec((CROWS, MAIN), lambda r, s, *_: (0, 0))
    return pl.pallas_call(
        coupling_kernel,
        out_shape=[jax.ShapeDtypeStruct((CROWS, MAIN), F32 if s == 0 else BF16) for s in range(4)],
        grid_spec=pltpu.PrefetchScalarGridSpec(
            num_scalar_prefetch=3,
            grid=(PAIR_DEV, PER_PAIR // n),
            in_specs=[pl.BlockSpec((1, n, NPNO, NPNO), lambda r, s, *_: (r, s, 0, 0))]
            + [any_spec] * 10,
            out_specs=[out] * 4,
            scratch_shapes=[
                pltpu.VMEM((TOTAL_ROWS, MAIN), BF16),
                pltpu.VMEM((PAIR_DEV, NPNO, NPNO), F32),
                pltpu.SemaphoreType.DMA((10,)),
            ],
        ),
        cost_estimate=pl.CostEstimate(
            flops=4 * 192 * 160**3, bytes_accessed=2 * (192 * 160 * 256 + TOTAL_ROWS * 128),
            transcendentals=0,
        ),
    )(z1, where, fock, margins, *blocks)


def update_kernel(last, count_ref, occ_ref, rows_ref, cols_ref, prev_ref, i0, i1, i2, i3, c0, c1, c2, c3, *outs):
    ints = [load_couple(ref, 0) for ref in (i0, i1, i2, i3)]
    cous = [load_couple(ref, 0) for ref in (c0, c1, c2, c3)]
    prev = load_couple(prev_ref, 0)
    new, res = [], []
    for i in range(2):
        whole = (ints[0][i] + ints[1][i]) + (ints[2][i] + ints[3][i])
        coupling = (cous[0][i] + cous[1][i]) + (cous[2][i] + cous[3][i])
        gap = rows_ref[i] + cols_ref[i] - occ_ref[i]
        keep = mask_of(count_ref[i])
        before = jnp.where(keep, prev[i], 0.0)
        residual = jnp.where(keep, whole - coupling + gap * before, 0.0)
        res.append(residual)
        new.append(before - residual / gap)
    if last:
        store_couple(outs[0], 0, *res)
    else:
        store_couple(outs[0], 0, *new)
        store_couple(outs[1], 0, *new)


def update(last, count2, occ2, rows2, cols2, prev, ints, cous):
    shapes = [jax.ShapeDtypeStruct((CROWS, MAIN), BF16)]
    if not last:
        shapes.append(jax.ShapeDtypeStruct((CROWS, MAIN), F32))
    vm = pl.BlockSpec(memory_space=VMEM)
    return pl.pallas_call(
        functools.partial(update_kernel, last),
        out_shape=shapes,
        in_specs=[pl.BlockSpec(memory_space=SMEM)] * 2 + [vm] * 11,
        out_specs=[vm] * len(shapes),
    )(count2, occ2, rows2, cols2, prev, *ints, *cous)


def final_kernel(z_ref, occ_ref, rows_ref, cols_ref, amp_ref, r0, r1, r2, r3, amp_out, res_out):
    z = z_ref[0]
    for s, ref in enumerate((r0, r1, r2, r3)):
        k = (z + s) % 4
        res = load_couple(ref, 0)
        amp = load_couple(amp_ref, s * CROWS)
        for i in range(2):
            pair = 2 * k + i
            gap = rows_ref[pair] + cols_ref[pair] - occ_ref[pair]
            res_out[pair] = res[i]
            amp_out[pair] = amp[i] - res[i] / gap


def final(z1, occ, rows, cols, amp, parts):
    vm = pl.BlockSpec(memory_space=VMEM)
    shape = jax.ShapeDtypeStruct((PAIR_DEV, NPNO, NPNO), F32)
    return pl.pallas_call(
        final_kernel,
        out_shape=[shape, shape],
        in_specs=[pl.BlockSpec(memory_space=SMEM)] * 2 + [vm] * 7,
        out_specs=[vm, vm],
    )(z1, occ, rows, cols, amp, *parts)


def scatter_fit(parts):
    return [parts[0]] + [send(parts[s], fit_shift(s)) for s in (1, 2, 3)]


def gather_fit(own):
    return [own] + [send(own, fit_shift(-s)) for s in (1, 2, 3)]


def shards(
    b_first,
    b_second,
    start_amplitudes,
    margins,
    fock_terms,
    partners,
    pno_energy,
    occ_energy,
    pair_list,
    pno_count,
):
    me = lax.axis_index("pairs")
    z = lax.axis_index("fit")
    z1 = z.astype(jnp.int32).reshape(1)
    packed = pack_start(z1, pno_count, start_amplitudes)
    where = locate(partners.reshape(-1), me, z)
    fock = fock_terms.reshape(-1)
    occ = occ_energy[pair_list[:, 0]] + occ_energy[pair_list[:, 1]]
    rows = pno_energy[:, :, None]
    cols = pno_energy[:, None, :]

    def own2(value):
        return lax.dynamic_slice_in_dim(value, 2 * z, 2, axis=0)

    fixed2 = (own2(pno_count), own2(occ), own2(rows), own2(cols))
    blocks = gather_blocks(packed)
    ints = scatter_fit(integral_parts(z1, b_first, b_second))
    start2 = own2(start_amplitudes)
    m0, m1, tail = pack_couple(start2[0], start2[1])
    prev = jnp.concatenate([m0, m1, tail])
    cous = scatter_fit(coupling_parts(z1, where, fock, margins, blocks))
    rounded, prev = update(False, *fixed2, prev, ints, cous)
    packed = jnp.concatenate(gather_fit(rounded))
    blocks = gather_blocks(packed)
    cous = scatter_fit(coupling_parts(z1, where, fock, margins, blocks))
    (res,) = update(True, *fixed2, prev, ints, cous)
    amplitudes, residual = final(z1, occ, rows, cols, packed, gather_fit(res))
    return (amplitudes, residual)


def solution(mesh):
    return jax.shard_map(
        shards,
        mesh=mesh,
        in_specs=(
            P("pairs", None, "fit"),
            P("pairs", None, "fit"),
            P("pairs", None, None),
            P("pairs", "fit", None, None),
            P("pairs", "fit"),
            P("pairs", "fit"),
            P("pairs", None),
            P(),
            P("pairs", None),
            P("pairs"),
        ),
        out_specs=(P("pairs", None, None), P("pairs", None, None)),
        check_vma=False,
    )
```

```python
import functools
import jax
import jax.numpy as jnp
from jax import lax
from jax.experimental import pallas as pl
from jax.experimental.pallas import tpu as pltpu
from jax.sharding import PartitionSpec as P

NPNO = 160
MAIN = 128
TAIL = NPNO - MAIN
PAIR_DEV = 8
COUPLES = 4
NFIT = 4
PER_PAIR = 24
FIT_DEV = 768
CROWS = 400
SHARD = COUPLES * CROWS
ROW4 = 4 * SHARD
UNIT = 24
VLIMIT = 34
ALL = ("pairs", "fit")
F32 = jnp.float32
BF16 = jnp.bfloat16
VMEM = pltpu.VMEM
SMEM = pltpu.SMEM


def lin(x, y, c, z):
    return ((x % 4) * 4 + (y % 4)) * 8 + c * 4 + (z % 4)


def device_list():
    return [(x, y, c, z) for x in range(4) for y in range(4) for c in range(2) for z in range(4)]


def ring(step, first):
    pairs = []
    for x, y, c, z in device_list():
        along_x = (c == 0) == first
        dx, dy = (step, 0) if along_x else (0, step)
        pairs.append((lin(x, y, c, z), lin(x + dx, y + dy, c, z)))
    return pairs


SWAP = [(lin(x, y, c, z), lin(x, y, 1 - c, z)) for x, y, c, z in device_list()]


def fit_shift(step):
    return [(lin(x, y, c, z), lin(x, y, c, z + step)) for x, y, c, z in device_list()]


def send(value, perm):
    return lax.ppermute(value, ALL, perm)


def locate(partners, me, z):
    x, y, c = me >> 3, (me >> 1) & 3, me & 1
    owner, local = partners >> 3, partners & 7
    oc = owner & 1
    dx, dy = ((owner >> 3) - x) & 3, ((owner >> 1) - y) & 3
    far = oc ^ c

    def place(distance):
        return jnp.where(distance == 3, 1, jnp.where(distance == 0, 0, distance + 1))

    slot_a = place(jnp.where(oc == 0, dx, dy))
    slot_b = place(jnp.where(oc == 0, dy, dx))
    side = (slot_b == 1) | (slot_b == 2)
    upper = jnp.where(side, 2 * far + slot_b + 1, jnp.where(slot_b == 0, far, 6 + far))
    couple = ((local >> 1) - z) & 3
    return (upper * ROW4 + slot_a * SHARD + couple * CROWS) * 2 + (local & 1)


def pack_couple(v0, v1):
    t = jnp.concatenate([v0[:, MAIN:], v1[:, MAIN:]], axis=1)
    tail = jnp.concatenate([t[:80], t[80:]], axis=1)
    return v0[:, :MAIN], v1[:, :MAIN], tail


def store_couple(ref, at, v0, v1):
    m0, m1, tail = pack_couple(v0, v1)
    ref[pl.ds(at, 160), :] = m0.astype(ref.dtype)
    ref[pl.ds(at + 160, 160), :] = m1.astype(ref.dtype)
    ref[pl.ds(at + 320, 80), :] = tail.astype(ref.dtype)


def load_couple(ref, at):
    m0 = ref[pl.ds(at, 160), :].astype(F32)
    m1 = ref[pl.ds(at + 160, 160), :].astype(F32)
    tail = ref[pl.ds(at + 320, 80), :].astype(F32)
    t = jnp.concatenate([tail[:, :64], tail[:, 64:]], axis=0)
    return (
        jnp.concatenate([m0, t[:, :TAIL]], axis=1),
        jnp.concatenate([m1, t[:, TAIL:]], axis=1),
    )


def mask_of(count):
    rows = lax.broadcasted_iota(jnp.int32, (NPNO, NPNO), 0)
    cols = lax.broadcasted_iota(jnp.int32, (NPNO, NPNO), 1)
    return (rows < count) & (cols < count)


def pack_kernel(at_ref, count_ref, start_ref, out_ref):
    z = at_ref[1]
    for k in range(COUPLES):
        slot = (k - z + 4) % 4
        v = [jnp.where(mask_of(count_ref[2 * k + i]), start_ref[2 * k + i], 0.0) for i in range(2)]
        store_couple(out_ref, pl.multiple_of(slot * CROWS, 16), *v)


def pack_start(at, count, start):
    return pl.pallas_call(
        pack_kernel,
        out_shape=jax.ShapeDtypeStruct((SHARD, MAIN), BF16),
        in_specs=[pl.BlockSpec(memory_space=SMEM)] * 2 + [pl.BlockSpec(memory_space=VMEM)],
        out_specs=pl.BlockSpec(memory_space=VMEM),
    )(at, count, start)


def fixed_kernel(at_ref, first_ref, second_ref, i0, i1, i2, i3):
    k = pl.program_id(0)
    v = [
        lax.dot_general(
            first_ref[i], second_ref[i], (((1,), (1,)), ((), ())), preferred_element_type=F32
        )
        for i in range(2)
    ]
    slot = (k - at_ref[1] + 4) % 4
    for s, ref in enumerate((i0, i1, i2, i3)):

        @pl.when(slot == s)
        def _():
            store_couple(ref, 0, *v)


def integral_parts(at, first, second):
    spec = pl.BlockSpec((2, NPNO, FIT_DEV), lambda k, z: (k, 0, 0))
    out = pl.BlockSpec((CROWS, MAIN), lambda k, z: (0, 0))
    return pl.pallas_call(
        fixed_kernel,
        out_shape=[jax.ShapeDtypeStruct((CROWS, MAIN), F32)] * 4,
        grid_spec=pltpu.PrefetchScalarGridSpec(
            num_scalar_prefetch=1, grid=(COUPLES,), in_specs=[spec, spec], out_specs=[out] * 4
        ),
        compiler_params=pltpu.CompilerParams(vmem_limit_bytes=8 * 2**20),
        cost_estimate=pl.CostEstimate(
            flops=2 * 8 * 160 * 160 * 768, bytes_accessed=4 * 8 * 160 * 768, transcendentals=0
        ),
    )(at, first, second)


def gap_kernel(at_ref, list_ref, occ_ref, energy_ref, partners_ref, out, where_out):
    where_out[...] = locate(partners_ref[...], at_ref[0], at_ref[1])
    for r in range(PAIR_DEV):
        line = jnp.broadcast_to(energy_ref[r : r + 1, :], (NPNO, NPNO))
        out[r] = line.T + line - (occ_ref[list_ref[0, r]] + occ_ref[list_ref[1, r]])


def make_gaps(at, pair_list, occ, energy, partners):
    smem = pl.BlockSpec(memory_space=SMEM)
    vmem = pl.BlockSpec(memory_space=VMEM)
    return pl.pallas_call(
        gap_kernel,
        out_shape=[
            jax.ShapeDtypeStruct((PAIR_DEV, NPNO, NPNO), F32),
            jax.ShapeDtypeStruct((PAIR_DEV, PER_PAIR), jnp.int32),
        ],
        in_specs=[smem, smem, smem, vmem, vmem],
        out_specs=[vmem, vmem],
        compiler_params=pltpu.CompilerParams(vmem_limit_bytes=8 * 2**20),
        cost_estimate=pl.CostEstimate(flops=10**6, bytes_accessed=4 * 10**6, transcendentals=0),
    )(at, pair_list.T, occ, energy, partners)


def products_kernel(at_ref, where_ref, fock_ref, margin_ref, block, *refs):
    outs, (acc, left) = refs[:4], refs[4:]
    r = pl.program_id(0)
    step = pl.program_id(1)

    def first_half(j):
        code = where_ref[r, step * UNIT + j]
        odd = code & 1
        base = pl.multiple_of(code >> 1, 16)
        main = block[pl.ds(pl.multiple_of(base + odd * 160, 16), 160), :]
        tail = block[pl.ds(pl.multiple_of(base + 320, 16), 80), :]
        wrapped = jnp.concatenate([tail[:, 64:], tail[:, :64]], axis=1)
        right = jnp.concatenate([main, jnp.concatenate([tail, wrapped], axis=0)], axis=1)
        value = jnp.dot(margin_ref[0, j], right, preferred_element_type=F32)
        rolled = pltpu.roll(value[:, MAIN:], odd * 96, axis=1)
        return jnp.concatenate([value[:, :MAIN], rolled[:, :TAIL]], axis=1).astype(BF16)

    def second_half(j, value):
        term = lax.dot_general(
            value, margin_ref[0, j], (((1,), (1,)), ((), ())), preferred_element_type=F32
        )
        return fock_ref[r, step * UNIT + j] * term

    total = None
    value = first_half(0)
    for j in range(UNIT):
        later = first_half(j + 1) if j + 1 < UNIT else None
        term = second_half(j, value)
        total = term if total is None else total + term
        value = later

    @pl.when(step == 0)
    def _():
        acc[r] = total

    @pl.when(step > 0)
    def _():
        acc[r] += total

    @pl.when((r == pl.num_programs(0) - 1) & (step == pl.num_programs(1) - 1))
    def _():
        z = at_ref[1]
        for s in range(NFIT):
            k = (z + s) % 4
            store_couple(outs[s], 0, acc[2 * k], acc[2 * k + 1])


def products(at, where, fock, margins, block):
    out = pl.BlockSpec((CROWS, MAIN), lambda r, s, *_: (0, 0))
    return pl.pallas_call(
        products_kernel,
        out_shape=[jax.ShapeDtypeStruct((CROWS, MAIN), F32 if s == 0 else BF16) for s in range(4)],
        grid_spec=pltpu.PrefetchScalarGridSpec(
            num_scalar_prefetch=3,
            grid=(PAIR_DEV, PER_PAIR // UNIT),
            in_specs=[
                pl.BlockSpec((1, UNIT, NPNO, NPNO), lambda r, s, *_: (r, s, 0, 0)),
                pl.BlockSpec(memory_space=VMEM),
            ],
            out_specs=[out] * 4,
            scratch_shapes=[
                pltpu.VMEM((PAIR_DEV, NPNO, NPNO), F32),
                pltpu.VMEM((8, 128), F32),
            ],
        ),
        compiler_params=pltpu.CompilerParams(vmem_limit_bytes=VLIMIT * 2**20),
        cost_estimate=pl.CostEstimate(
            flops=192 * 16 * 160**3, bytes_accessed=192 * 2 * 160 * 256, transcendentals=0
        ),
    )(at, where, fock, margins, block)


def update_kernel(last, own_at, *refs):
    at_ref, count_ref, gap_ref, prev_ref = refs[:4]
    ints, cous, outs = refs[4:8], refs[8:12], refs[12:]
    z = at_ref[1]
    ints = [load_couple(ref, 0) for ref in ints]
    cous = [load_couple(ref, 0) for ref in cous]
    new, res = [], []
    for i in range(2):
        pair = 2 * z + i
        whole = (ints[0][i] + ints[1][i]) + (ints[2][i] + ints[3][i])
        coupling = (cous[0][i] + cous[1][i]) + (cous[2][i] + cous[3][i])
        gap = gap_ref[pair]
        keep = mask_of(count_ref[pair])
        before = jnp.where(keep, prev_ref[pair if own_at else i], 0.0)
        residual = jnp.where(keep, whole - coupling + gap * before, 0.0)
        res.append(residual)
        new.append(before - residual / gap)
    if last:
        store_couple(outs[0], 0, *res)
    else:
        store_couple(outs[0], 0, *new)
        for i in range(2):
            outs[1][i] = new[i]


def update(last, at, count, gaps, prev, ints, cous):
    shapes = [jax.ShapeDtypeStruct((CROWS, MAIN), BF16)]
    if not last:
        shapes.append(jax.ShapeDtypeStruct((2, NPNO, NPNO), F32))
    vm = pl.BlockSpec(memory_space=VMEM)
    return pl.pallas_call(
        functools.partial(update_kernel, last, prev.shape[0] == PAIR_DEV),
        out_shape=shapes,
        in_specs=[pl.BlockSpec(memory_space=SMEM)] * 2 + [vm] * 10,
        out_specs=[vm] * len(shapes),
    )(at, count, gaps, prev, *ints, *cous)


def final_kernel(at_ref, gap_ref, amp_ref, r0, r1, r2, r3, amp_out, res_out):
    z = at_ref[1]
    for s, ref in enumerate((r0, r1, r2, r3)):
        k = (z + s) % 4
        res = load_couple(ref, 0)
        amp = load_couple(amp_ref, s * CROWS)
        for i in range(2):
            pair = 2 * k + i
            res_out[pair] = res[i]
            amp_out[pair] = amp[i] - res[i] / gap_ref[pair]


def final(at, gaps, amp, parts):
    vm = pl.BlockSpec(memory_space=VMEM)
    shape = jax.ShapeDtypeStruct((PAIR_DEV, NPNO, NPNO), F32)
    return pl.pallas_call(
        final_kernel,
        out_shape=[shape, shape],
        in_specs=[pl.BlockSpec(memory_space=SMEM)] + [vm] * 6,
        out_specs=[vm, vm],
    )(at, gaps, amp, *parts)


def scatter_fit(parts):
    return [parts[0]] + [send(parts[s], fit_shift(s)) for s in (1, 2, 3)]


def gather_fit(own):
    return [own] + [send(own, fit_shift(-s)) for s in (1, 2, 3)]


def coupling_of(shard, at, margins, prepare):
    half = SHARD // 2
    near_p = send(shard, ring(1, True))
    near_m = send(shard, ring(-1, True))
    far_p = send(near_p[:half], ring(1, True))
    far_m = send(near_m[half:], ring(-1, True))
    row = jnp.concatenate([shard, near_p, near_m, far_p, far_m])
    next_p = send(row, ring(1, False))
    next_m = send(row, ring(-1, False))
    row_x = send(row, SWAP)
    side = prepare()
    next_p, next_m, side = lax.optimization_barrier((next_p, next_m, side))
    half = ROW4 // 2
    last_p = send(next_p[:half], ring(1, False))
    last_m = send(next_m[half:], ring(-1, False))
    next_p_x = send(next_p, SWAP)
    next_m_x = send(next_m, SWAP)
    last_p_x = send(last_p, SWAP)
    last_m_x = send(last_m, SWAP)
    block = jnp.concatenate(
        [row, row_x, next_p, next_m, next_p_x, next_m_x, last_p, last_m, last_p_x, last_m_x]
    )
    parts = products(at, side[0], side[1], margins, block)
    return scatter_fit(parts), side


def shards(
    b_first,
    b_second,
    start_amplitudes,
    margins,
    fock_terms,
    partners,
    pno_energy,
    occ_energy,
    pair_list,
    pno_count,
):
    at = jnp.stack([lax.axis_index("pairs"), lax.axis_index("fit")]).astype(jnp.int32)
    packed = pack_start(at, pno_count, start_amplitudes)

    def prepare():
        gaps, where = make_gaps(at, pair_list, occ_energy, pno_energy, partners)
        ints = scatter_fit(integral_parts(at, b_first, b_second))
        return where, fock_terms, ints, gaps

    cous, side = coupling_of(packed, at, margins, prepare)
    ints, gaps = side[2:]
    rounded, prev = update(False, at, pno_count, gaps, start_amplitudes, ints, cous)
    packed = jnp.concatenate(gather_fit(rounded))
    cous, _ = coupling_of(packed, at, margins, lambda: side)
    (res,) = update(True, at, pno_count, gaps, prev, ints, cous)
    amplitudes, residual = final(at, gaps, packed, gather_fit(res))
    return (amplitudes, residual)


def solution(mesh):
    return jax.shard_map(
        shards,
        mesh=mesh,
        in_specs=(
            P("pairs", None, "fit"),
            P("pairs", None, "fit"),
            P("pairs", None, None),
            P("pairs", "fit", None, None),
            P("pairs", "fit"),
            P("pairs", "fit"),
            P("pairs", None),
            P(),
            P("pairs", None),
            P("pairs"),
        ),
        out_specs=(P("pairs", None, None), P("pairs", None, None)),
        check_vma=False,
    )
```

```python
import functools
import jax
import jax.numpy as jnp
from jax import lax
from jax.experimental import pallas as pl
from jax.experimental.pallas import tpu as pltpu
from jax.sharding import PartitionSpec as P

NPNO = 160
MAIN = 128
TAIL = NPNO - MAIN
PAIR_DEV = 8
COUPLES = 4
NFIT = 4
PER_PAIR = 24
FIT_DEV = 768
CROWS = 400
SHARD = COUPLES * CROWS
ROW4 = 4 * SHARD
UNIT = 24
GRANTS = (34, 29)
ALL = ("pairs", "fit")
F32 = jnp.float32
BF16 = jnp.bfloat16
VMEM = pltpu.VMEM
SMEM = pltpu.SMEM


def lin(x, y, c, z):
    return ((x % 4) * 4 + (y % 4)) * 8 + c * 4 + (z % 4)


def device_list():
    return [(x, y, c, z) for x in range(4) for y in range(4) for c in range(2) for z in range(4)]


def ring(step, first):
    pairs = []
    for x, y, c, z in device_list():
        along_x = (c == 0) == first
        dx, dy = (step, 0) if along_x else (0, step)
        pairs.append((lin(x, y, c, z), lin(x + dx, y + dy, c, z)))
    return pairs


SWAP = [(lin(x, y, c, z), lin(x, y, 1 - c, z)) for x, y, c, z in device_list()]


def fit_shift(step):
    return [(lin(x, y, c, z), lin(x, y, c, z + step)) for x, y, c, z in device_list()]


def send(value, perm):
    return lax.ppermute(value, ALL, perm)


def locate(partners, me, z):
    x, y, c = me >> 3, (me >> 1) & 3, me & 1
    owner, local = partners >> 3, partners & 7
    oc = owner & 1
    dx, dy = ((owner >> 3) - x) & 3, ((owner >> 1) - y) & 3
    far = oc ^ c

    def place(distance):
        return jnp.where(distance == 3, 1, jnp.where(distance == 0, 0, distance + 1))

    slot_a = place(jnp.where(oc == 0, dx, dy))
    slot_b = place(jnp.where(oc == 0, dy, dx))
    side = (slot_b == 1) | (slot_b == 2)
    upper = jnp.where(side, 2 * far + slot_b + 1, jnp.where(slot_b == 0, far, 6 + far))
    couple = ((local >> 1) - z) & 3
    return (upper * ROW4 + slot_a * SHARD + couple * CROWS) * 2 + (local & 1)


def pack_couple(v0, v1):
    t = jnp.concatenate([v0[:, MAIN:], v1[:, MAIN:]], axis=1)
    tail = jnp.concatenate([t[:80], t[80:]], axis=1)
    return v0[:, :MAIN], v1[:, :MAIN], tail


def store_couple(ref, at, v0, v1):
    m0, m1, tail = pack_couple(v0, v1)
    ref[pl.ds(at, 160), :] = m0.astype(ref.dtype)
    ref[pl.ds(at + 160, 160), :] = m1.astype(ref.dtype)
    ref[pl.ds(at + 320, 80), :] = tail.astype(ref.dtype)


def load_couple(ref, at):
    m0 = ref[pl.ds(at, 160), :].astype(F32)
    m1 = ref[pl.ds(at + 160, 160), :].astype(F32)
    tail = ref[pl.ds(at + 320, 80), :].astype(F32)
    t = jnp.concatenate([tail[:, :64], tail[:, 64:]], axis=0)
    return (
        jnp.concatenate([m0, t[:, :TAIL]], axis=1),
        jnp.concatenate([m1, t[:, TAIL:]], axis=1),
    )


def mask_of(count):
    rows = lax.broadcasted_iota(jnp.int32, (NPNO, NPNO), 0)
    cols = lax.broadcasted_iota(jnp.int32, (NPNO, NPNO), 1)
    return (rows < count) & (cols < count)


def pack_kernel(at_ref, count_ref, start_ref, out_ref):
    z = at_ref[1]
    for k in range(COUPLES):
        slot = (k - z + 4) % 4
        v = [jnp.where(mask_of(count_ref[2 * k + i]), start_ref[2 * k + i], 0.0) for i in range(2)]
        store_couple(out_ref, pl.multiple_of(slot * CROWS, 16), *v)


def pack_start(at, count, start):
    return pl.pallas_call(
        pack_kernel,
        out_shape=jax.ShapeDtypeStruct((SHARD, MAIN), BF16),
        in_specs=[pl.BlockSpec(memory_space=SMEM)] * 2 + [pl.BlockSpec(memory_space=VMEM)],
        out_specs=pl.BlockSpec(memory_space=VMEM),
        compiler_params=pltpu.CompilerParams(vmem_limit_bytes=8 * 2**20),
    )(at, count, start)


def fixed_kernel(at_ref, first_ref, second_ref, i0, i1, i2, i3):
    k = pl.program_id(0)
    v = [
        lax.dot_general(
            first_ref[i], second_ref[i], (((1,), (1,)), ((), ())), preferred_element_type=F32
        )
        for i in range(2)
    ]
    slot = (k - at_ref[1] + 4) % 4
    for s, ref in enumerate((i0, i1, i2, i3)):

        @pl.when(slot == s)
        def _():
            store_couple(ref, 0, *v)


def integral_parts(at, first, second):
    spec = pl.BlockSpec((2, NPNO, FIT_DEV), lambda k, z: (k, 0, 0))
    out = pl.BlockSpec((CROWS, MAIN), lambda k, z: (0, 0))
    return pl.pallas_call(
        fixed_kernel,
        out_shape=[jax.ShapeDtypeStruct((CROWS, MAIN), F32)] * 4,
        grid_spec=pltpu.PrefetchScalarGridSpec(
            num_scalar_prefetch=1, grid=(COUPLES,), in_specs=[spec, spec], out_specs=[out] * 4
        ),
        compiler_params=pltpu.CompilerParams(vmem_limit_bytes=8 * 2**20),
        cost_estimate=pl.CostEstimate(
            flops=2 * 8 * 160 * 160 * 768, bytes_accessed=4 * 8 * 160 * 768, transcendentals=0
        ),
    )(at, first, second)


def table_kernel(
    at_ref,
    list_ref,
    count_ref,
    occ_ref,
    energy_ref,
    partners_ref,
    start_ref,
    where_out,
    inverse_out,
    gap_out,
    inverse2_out,
    keep_out,
    start_out,
):
    z = at_ref[1]
    where_out[...] = locate(partners_ref[...], at_ref[0], z)

    def gap_of(r, line):
        line = jnp.broadcast_to(line, (NPNO, NPNO))
        return line.T + line - (occ_ref[list_ref[0, r]] + occ_ref[list_ref[1, r]])

    for r in range(PAIR_DEV):
        inverse_out[r] = 1.0 / gap_of(r, energy_ref[r : r + 1, :])
    own = [2 * z, 2 * z + 1]
    gaps = [gap_of(r, energy_ref[pl.ds(r, 1), :]) for r in own]
    keep = [mask_of(count_ref[r]) for r in own]
    store_couple(gap_out, 0, *gaps)
    store_couple(inverse2_out, 0, *[1.0 / gap for gap in gaps])
    store_couple(keep_out, 0, *[jnp.where(k, 1.0, 0.0) for k in keep])
    store_couple(start_out, 0, *[jnp.where(k, start_ref[r], 0.0) for r, k in zip(own, keep)])


def make_tables(at, pair_list, count, occ, energy, partners, start):
    smem = pl.BlockSpec(memory_space=SMEM)
    vmem = pl.BlockSpec(memory_space=VMEM)
    packed = jax.ShapeDtypeStruct((CROWS, MAIN), F32)
    return pl.pallas_call(
        table_kernel,
        out_shape=[
            jax.ShapeDtypeStruct((PAIR_DEV, PER_PAIR), jnp.int32),
            jax.ShapeDtypeStruct((PAIR_DEV, NPNO, NPNO), F32),
        ]
        + [packed] * 4,
        in_specs=[smem] * 4 + [vmem] * 3,
        out_specs=[vmem] * 6,
        compiler_params=pltpu.CompilerParams(vmem_limit_bytes=10 * 2**20),
        cost_estimate=pl.CostEstimate(flops=10**6, bytes_accessed=6 * 10**6, transcendentals=0),
    )(at, pair_list.T, count, occ, energy, partners, start)


def products_kernel(at_ref, where_ref, fock_ref, margin_ref, block, *refs):
    outs, (acc, left) = refs[:4], refs[4:]
    r = pl.program_id(0)
    step = pl.program_id(1)

    def first_half(j):
        code = where_ref[r, step * UNIT + j]
        odd = code & 1
        base = pl.multiple_of(code >> 1, 16)
        main = block[pl.ds(pl.multiple_of(base + odd * 160, 16), 160), :]
        tail = block[pl.ds(pl.multiple_of(base + 320, 16), 80), :]
        wrapped = jnp.concatenate([tail[:, 64:], tail[:, :64]], axis=1)
        right = jnp.concatenate([main, jnp.concatenate([tail, wrapped], axis=0)], axis=1)
        value = jnp.dot(margin_ref[0, j], right, preferred_element_type=F32)
        rolled = pltpu.roll(value[:, MAIN:], odd * 96, axis=1)
        return jnp.concatenate([value[:, :MAIN], rolled[:, :TAIL]], axis=1).astype(BF16)

    def second_half(j, value):
        term = lax.dot_general(
            value, margin_ref[0, j], (((1,), (1,)), ((), ())), preferred_element_type=F32
        )
        return fock_ref[r, step * UNIT + j] * term

    total = None
    value = first_half(0)
    for j in range(UNIT):
        later = first_half(j + 1) if j + 1 < UNIT else None
        term = second_half(j, value)
        total = term if total is None else total + term
        value = later

    @pl.when(step == 0)
    def _():
        acc[r] = total

    @pl.when(step > 0)
    def _():
        acc[r] += total

    @pl.when((r == pl.num_programs(0) - 1) & (step == pl.num_programs(1) - 1))
    def _():
        z = at_ref[1]
        for s in range(NFIT):
            k = (z + s) % 4
            store_couple(outs[s], 0, acc[2 * k], acc[2 * k + 1])


def products(at, where, fock, margins, block, grant):
    out = pl.BlockSpec((CROWS, MAIN), lambda r, s, *_: (0, 0))
    return pl.pallas_call(
        products_kernel,
        out_shape=[jax.ShapeDtypeStruct((CROWS, MAIN), F32 if s == 0 else BF16) for s in range(4)],
        grid_spec=pltpu.PrefetchScalarGridSpec(
            num_scalar_prefetch=3,
            grid=(PAIR_DEV, PER_PAIR // UNIT),
            in_specs=[
                pl.BlockSpec((1, UNIT, NPNO, NPNO), lambda r, s, *_: (r, s, 0, 0)),
                pl.BlockSpec(memory_space=VMEM),
            ],
            out_specs=[out] * 4,
            scratch_shapes=[
                pltpu.VMEM((PAIR_DEV, NPNO, NPNO), F32),
                pltpu.VMEM((8, 128), F32),
            ],
        ),
        compiler_params=pltpu.CompilerParams(vmem_limit_bytes=grant * 2**20),
        cost_estimate=pl.CostEstimate(
            flops=192 * 16 * 160**3, bytes_accessed=192 * 2 * 160 * 256, transcendentals=0
        ),
    )(at, where, fock, margins, block)


def update_kernel(last, keep_ref, gap_ref, inverse_ref, prev_ref, *refs):
    i0, i1, i2, i3, c0, c1, c2, c3 = [ref[...].astype(F32) for ref in refs[:8]]
    outs = refs[8:]
    whole = (i0 + i1) + (i2 + i3)
    coupling = (c0 + c1) + (c2 + c3)
    before = prev_ref[...]
    residual = keep_ref[...] * (whole - coupling + gap_ref[...] * before)
    if last:
        outs[0][...] = residual.astype(BF16)
    else:
        new = before - residual * inverse_ref[...]
        outs[0][...] = new.astype(BF16)
        outs[1][...] = new


def update(last, tables, prev, ints, cous):
    shapes = [jax.ShapeDtypeStruct((CROWS, MAIN), BF16)]
    if not last:
        shapes.append(jax.ShapeDtypeStruct((CROWS, MAIN), F32))
    vm = pl.BlockSpec(memory_space=VMEM)
    return pl.pallas_call(
        functools.partial(update_kernel, last),
        out_shape=shapes,
        in_specs=[vm] * 12,
        out_specs=[vm] * len(shapes),
        compiler_params=pltpu.CompilerParams(vmem_limit_bytes=6 * 2**20),
    )(*tables, prev, *ints, *cous)


def final_kernel(at_ref, inverse_ref, amp_ref, r0, r1, r2, r3, amp_out, res_out):
    z = at_ref[1]
    for s, ref in enumerate((r0, r1, r2, r3)):
        k = (z + s) % 4
        res = load_couple(ref, 0)
        amp = load_couple(amp_ref, s * CROWS)
        for i in range(2):
            pair = 2 * k + i
            res_out[pair] = res[i]
            amp_out[pair] = amp[i] - res[i] * inverse_ref[pair]


def final(at, inverse, amp, parts):
    vm = pl.BlockSpec(memory_space=VMEM)
    shape = jax.ShapeDtypeStruct((PAIR_DEV, NPNO, NPNO), F32)
    return pl.pallas_call(
        final_kernel,
        out_shape=[shape, shape],
        in_specs=[pl.BlockSpec(memory_space=SMEM)] + [vm] * 6,
        out_specs=[vm, vm],
        compiler_params=pltpu.CompilerParams(vmem_limit_bytes=16 * 2**20),
    )(at, inverse, amp, *parts)


def scatter_fit(parts):
    return [parts[0]] + [send(parts[s], fit_shift(s)) for s in (1, 2, 3)]


def gather_fit(own):
    return [own] + [send(own, fit_shift(-s)) for s in (1, 2, 3)]


def coupling_of(shard, at, margins, prepare, grant):
    half = SHARD // 2
    near_p = send(shard, ring(1, True))
    near_m = send(shard, ring(-1, True))
    far_p = send(near_p[:half], ring(1, True))
    far_m = send(near_m[half:], ring(-1, True))
    row = jnp.concatenate([shard, near_p, near_m, far_p, far_m])
    next_p = send(row, ring(1, False))
    next_m = send(row, ring(-1, False))
    row_x = send(row, SWAP)
    side = prepare()
    next_p, next_m, side = lax.optimization_barrier((next_p, next_m, side))
    half = ROW4 // 2
    last_p = send(next_p[:half], ring(1, False))
    last_m = send(next_m[half:], ring(-1, False))
    next_p_x = send(next_p, SWAP)
    next_m_x = send(next_m, SWAP)
    last_p_x = send(last_p, SWAP)
    last_m_x = send(last_m, SWAP)
    block = jnp.concatenate(
        [row, row_x, next_p, next_m, next_p_x, next_m_x, last_p, last_m, last_p_x, last_m_x]
    )
    parts = products(at, side[0], side[1], margins, block, grant)
    return scatter_fit(parts), side


def shards(
    b_first,
    b_second,
    start_amplitudes,
    margins,
    fock_terms,
    partners,
    pno_energy,
    occ_energy,
    pair_list,
    pno_count,
):
    at = jnp.stack([lax.axis_index("pairs"), lax.axis_index("fit")]).astype(jnp.int32)
    packed = pack_start(at, pno_count, start_amplitudes)

    def prepare():
        where, *tables = make_tables(
            at, pair_list, pno_count, occ_energy, pno_energy, partners, start_amplitudes
        )
        ints = scatter_fit(integral_parts(at, b_first, b_second))
        return where, fock_terms, ints, tables

    cous, side = coupling_of(packed, at, margins, prepare, GRANTS[0])
    ints, (inverse, gap2, inverse2, keep2, start2) = side[2:]
    tables = (keep2, gap2, inverse2)
    rounded, prev = update(False, tables, start2, ints, cous)
    packed = jnp.concatenate(gather_fit(rounded))
    cous, _ = coupling_of(packed, at, margins, lambda: side, GRANTS[1])
    (res,) = update(True, tables, prev, ints, cous)
    amplitudes, residual = final(at, inverse, packed, gather_fit(res))
    return (amplitudes, residual)


def solution(mesh):
    return jax.shard_map(
        shards,
        mesh=mesh,
        in_specs=(
            P("pairs", None, "fit"),
            P("pairs", None, "fit"),
            P("pairs", None, None),
            P("pairs", "fit", None, None),
            P("pairs", "fit"),
            P("pairs", "fit"),
            P("pairs", None),
            P(),
            P("pairs", None),
            P("pairs"),
        ),
        out_specs=(P("pairs", None, None), P("pairs", None, None)),
        check_vma=False,
    )
```

```python
import functools
import jax
import jax.numpy as jnp
from jax import lax
from jax.experimental import pallas as pl
from jax.experimental.pallas import tpu as pltpu
from jax.sharding import PartitionSpec as P

NPNO = 160
MAIN = 128
TAIL = NPNO - MAIN
PAIR_DEV = 8
COUPLES = 4
NFIT = 4
PER_PAIR = 24
FIT_DEV = 768
CROWS = 400
SHARD = COUPLES * CROWS
ROW4 = 4 * SHARD
UNIT = 24
GRANTS = (34, 29)
ALL = ("pairs", "fit")
F32 = jnp.float32
BF16 = jnp.bfloat16
VMEM = pltpu.VMEM
SMEM = pltpu.SMEM


def lin(x, y, c, z):
    return ((x % 4) * 4 + (y % 4)) * 8 + c * 4 + (z % 4)


def device_list():
    return [(x, y, c, z) for x in range(4) for y in range(4) for c in range(2) for z in range(4)]


def ring(step, first):
    pairs = []
    for x, y, c, z in device_list():
        along_x = (c == 0) == first
        dx, dy = (step, 0) if along_x else (0, step)
        pairs.append((lin(x, y, c, z), lin(x + dx, y + dy, c, z)))
    return pairs


SWAP = [(lin(x, y, c, z), lin(x, y, 1 - c, z)) for x, y, c, z in device_list()]


def fit_shift(step):
    return [(lin(x, y, c, z), lin(x, y, c, z + step)) for x, y, c, z in device_list()]


def send(value, perm):
    return lax.ppermute(value, ALL, perm)


def locate(partners, me, z):
    x, y, c = me >> 3, (me >> 1) & 3, me & 1
    owner, local = partners >> 3, partners & 7
    oc = owner & 1
    dx, dy = ((owner >> 3) - x) & 3, ((owner >> 1) - y) & 3
    far = oc ^ c

    def place(distance):
        return jnp.where(distance == 3, 1, jnp.where(distance == 0, 0, distance + 1))

    slot_a = place(jnp.where(oc == 0, dx, dy))
    slot_b = place(jnp.where(oc == 0, dy, dx))
    side = (slot_b == 1) | (slot_b == 2)
    upper = jnp.where(side, 2 * far + slot_b + 1, jnp.where(slot_b == 0, far, 6 + far))
    couple = ((local >> 1) - z) & 3
    return (upper * ROW4 + slot_a * SHARD + couple * CROWS) * 2 + (local & 1)


def pack_couple(v0, v1):
    t = jnp.concatenate([v0[:, MAIN:], v1[:, MAIN:]], axis=1)
    tail = jnp.concatenate([t[:80], t[80:]], axis=1)
    return v0[:, :MAIN], v1[:, :MAIN], tail


def store_couple(ref, at, v0, v1):
    m0, m1, tail = pack_couple(v0, v1)
    ref[pl.ds(at, 160), :] = m0.astype(ref.dtype)
    ref[pl.ds(at + 160, 160), :] = m1.astype(ref.dtype)
    ref[pl.ds(at + 320, 80), :] = tail.astype(ref.dtype)


def load_couple(ref, at):
    m0 = ref[pl.ds(at, 160), :].astype(F32)
    m1 = ref[pl.ds(at + 160, 160), :].astype(F32)
    tail = ref[pl.ds(at + 320, 80), :].astype(F32)
    t = jnp.concatenate([tail[:, :64], tail[:, 64:]], axis=0)
    return (
        jnp.concatenate([m0, t[:, :TAIL]], axis=1),
        jnp.concatenate([m1, t[:, TAIL:]], axis=1),
    )


def mask_of(count):
    rows = lax.broadcasted_iota(jnp.int32, (NPNO, NPNO), 0)
    cols = lax.broadcasted_iota(jnp.int32, (NPNO, NPNO), 1)
    return (rows < count) & (cols < count)


def pack_kernel(at_ref, count_ref, start_ref, out_ref):
    z = at_ref[1]
    for k in range(COUPLES):
        slot = (k - z + 4) % 4
        v = [jnp.where(mask_of(count_ref[2 * k + i]), start_ref[2 * k + i], 0.0) for i in range(2)]
        store_couple(out_ref, pl.multiple_of(slot * CROWS, 16), *v)


def pack_start(at, count, start):
    return pl.pallas_call(
        pack_kernel,
        out_shape=jax.ShapeDtypeStruct((SHARD, MAIN), BF16),
        in_specs=[pl.BlockSpec(memory_space=SMEM)] * 2 + [pl.BlockSpec(memory_space=VMEM)],
        out_specs=pl.BlockSpec(memory_space=VMEM),
        compiler_params=pltpu.CompilerParams(vmem_limit_bytes=8 * 2**20),
    )(at, count, start)


def fixed_kernel(at_ref, first_ref, second_ref, i0, i1, i2, i3):
    k = pl.program_id(0)
    v = [
        lax.dot_general(
            first_ref[i], second_ref[i], (((1,), (1,)), ((), ())), preferred_element_type=F32
        )
        for i in range(2)
    ]
    slot = (k - at_ref[1] + 4) % 4
    for s, ref in enumerate((i0, i1, i2, i3)):

        @pl.when(slot == s)
        def _():
            store_couple(ref, 0, *v)


def integral_parts(at, first, second):
    spec = pl.BlockSpec((2, NPNO, FIT_DEV), lambda k, z: (k, 0, 0))
    out = pl.BlockSpec((CROWS, MAIN), lambda k, z: (0, 0))
    return pl.pallas_call(
        fixed_kernel,
        out_shape=[jax.ShapeDtypeStruct((CROWS, MAIN), F32)] * 4,
        grid_spec=pltpu.PrefetchScalarGridSpec(
            num_scalar_prefetch=1, grid=(COUPLES,), in_specs=[spec, spec], out_specs=[out] * 4
        ),
        compiler_params=pltpu.CompilerParams(vmem_limit_bytes=8 * 2**20),
        cost_estimate=pl.CostEstimate(
            flops=2 * 8 * 160 * 160 * 768, bytes_accessed=4 * 8 * 160 * 768, transcendentals=0
        ),
    )(at, first, second)


def table_kernel(
    at_ref,
    list_ref,
    count_ref,
    occ_ref,
    energy_ref,
    partners_ref,
    start_ref,
    where_out,
    inverse_out,
    gap_out,
    inverse2_out,
    keep_out,
    start_out,
):
    z = at_ref[1]
    where_out[...] = locate(partners_ref[...], at_ref[0], z)

    def gap_of(r, line):
        line = jnp.broadcast_to(line, (NPNO, NPNO))
        return line.T + line - (occ_ref[list_ref[0, r]] + occ_ref[list_ref[1, r]])

    for r in range(PAIR_DEV):
        inverse_out[r] = 1.0 / gap_of(r, energy_ref[r : r + 1, :])
    own = [2 * z, 2 * z + 1]
    gaps = [gap_of(r, energy_ref[pl.ds(r, 1), :]) for r in own]
    keep = [mask_of(count_ref[r]) for r in own]
    store_couple(gap_out, 0, *gaps)
    store_couple(inverse2_out, 0, *[1.0 / gap for gap in gaps])
    store_couple(keep_out, 0, *[jnp.where(k, 1.0, 0.0) for k in keep])
    store_couple(start_out, 0, *[jnp.where(k, start_ref[r], 0.0) for r, k in zip(own, keep)])


def make_tables(at, pair_list, count, occ, energy, partners, start):
    smem = pl.BlockSpec(memory_space=SMEM)
    vmem = pl.BlockSpec(memory_space=VMEM)
    packed = jax.ShapeDtypeStruct((CROWS, MAIN), F32)
    return pl.pallas_call(
        table_kernel,
        out_shape=[
            jax.ShapeDtypeStruct((PAIR_DEV, PER_PAIR), jnp.int32),
            jax.ShapeDtypeStruct((PAIR_DEV, NPNO, NPNO), F32),
        ]
        + [packed] * 4,
        in_specs=[smem] * 4 + [vmem] * 3,
        out_specs=[vmem] * 6,
        compiler_params=pltpu.CompilerParams(vmem_limit_bytes=10 * 2**20),
        cost_estimate=pl.CostEstimate(flops=10**6, bytes_accessed=6 * 10**6, transcendentals=0),
    )(at, pair_list.T, count, occ, energy, partners, start)


def row_of(own, r, at_ref):
    g = r >> 1
    shift = 0 if own else jnp.where(g == 0, 2, 2 * g - 1)
    return 2 * ((at_ref[1] + shift) & 3) + (r & 1)


def products_kernel(own, at_ref, where_ref, fock_ref, margin_ref, block, *refs):
    outs, acc = refs[:-1], refs[-1]
    at = pl.program_id(0)
    r = row_of(own, at, at_ref)

    def first_half(j):
        code = where_ref[r, j]
        odd = code & 1
        base = pl.multiple_of(code >> 1, 16)
        main = block[pl.ds(pl.multiple_of(base + odd * 160, 16), 160), :]
        tail = block[pl.ds(pl.multiple_of(base + 320, 16), 80), :]
        wrapped = jnp.concatenate([tail[:, 64:], tail[:, :64]], axis=1)
        right = jnp.concatenate([main, jnp.concatenate([tail, wrapped], axis=0)], axis=1)
        value = jnp.dot(margin_ref[0, j], right, preferred_element_type=F32)
        rolled = pltpu.roll(value[:, MAIN:], odd * 96, axis=1)
        return jnp.concatenate([value[:, :MAIN], rolled[:, :TAIL]], axis=1).astype(BF16)

    def second_half(j, value):
        term = lax.dot_general(
            value, margin_ref[0, j], (((1,), (1,)), ((), ())), preferred_element_type=F32
        )
        return fock_ref[r, j] * term

    total = None
    value = first_half(0)
    for j in range(UNIT):
        later = first_half(j + 1) if j + 1 < UNIT else None
        term = second_half(j, value)
        total = term if total is None else total + term
        value = later

    acc[at] = total

    @pl.when(at == pl.num_programs(0) - 1)
    def _():
        for i, out in enumerate(outs):
            store_couple(out, 0, acc[2 * i], acc[2 * i + 1])


def products(own, at, where, fock, margins, block, grant):
    out = pl.BlockSpec((CROWS, MAIN), lambda r, *_: (0, 0))
    n = 1 if own else 3
    return pl.pallas_call(
        functools.partial(products_kernel, own),
        out_shape=[jax.ShapeDtypeStruct((CROWS, MAIN), F32 if own else BF16)] * n,
        grid_spec=pltpu.PrefetchScalarGridSpec(
            num_scalar_prefetch=3,
            grid=(2 * n,),
            in_specs=[
                pl.BlockSpec(
                    (1, UNIT, NPNO, NPNO), lambda r, at, *_: (row_of(own, r, at), 0, 0, 0)
                ),
                pl.BlockSpec(memory_space=VMEM),
            ],
            out_specs=[out] * n,
            scratch_shapes=[pltpu.VMEM((2 * n, NPNO, NPNO), F32)],
        ),
        compiler_params=pltpu.CompilerParams(vmem_limit_bytes=grant * 2**20),
        cost_estimate=pl.CostEstimate(
            flops=n * 48 * 16 * 160**3, bytes_accessed=n * 48 * 2 * 160 * 256, transcendentals=0
        ),
    )(at, where, fock, margins, block)


def update_kernel(last, keep_ref, gap_ref, inverse_ref, prev_ref, *refs):
    i0, i1, i2, i3, c0, c1, c2, c3 = [ref[...].astype(F32) for ref in refs[:8]]
    outs = refs[8:]
    whole = (i0 + i1) + (i2 + i3)
    coupling = (c0 + c1) + (c2 + c3)
    before = prev_ref[...]
    residual = keep_ref[...] * (whole - coupling + gap_ref[...] * before)
    if last:
        outs[0][...] = residual.astype(BF16)
    else:
        new = before - residual * inverse_ref[...]
        outs[0][...] = new.astype(BF16)
        outs[1][...] = new


def update(last, tables, prev, ints, cous):
    shapes = [jax.ShapeDtypeStruct((CROWS, MAIN), BF16)]
    if not last:
        shapes.append(jax.ShapeDtypeStruct((CROWS, MAIN), F32))
    vm = pl.BlockSpec(memory_space=VMEM)
    return pl.pallas_call(
        functools.partial(update_kernel, last),
        out_shape=shapes,
        in_specs=[vm] * 12,
        out_specs=[vm] * len(shapes),
        compiler_params=pltpu.CompilerParams(vmem_limit_bytes=6 * 2**20),
    )(*tables, prev, *ints, *cous)


def final_kernel(at_ref, inverse_ref, amp_ref, r0, r1, r2, r3, amp_out, res_out):
    z = at_ref[1]
    for s, ref in enumerate((r0, r1, r2, r3)):
        k = (z + s) % 4
        res = load_couple(ref, 0)
        amp = load_couple(amp_ref, s * CROWS)
        for i in range(2):
            pair = 2 * k + i
            res_out[pair] = res[i]
            amp_out[pair] = amp[i] - res[i] * inverse_ref[pair]


def final(at, inverse, amp, parts):
    vm = pl.BlockSpec(memory_space=VMEM)
    shape = jax.ShapeDtypeStruct((PAIR_DEV, NPNO, NPNO), F32)
    return pl.pallas_call(
        final_kernel,
        out_shape=[shape, shape],
        in_specs=[pl.BlockSpec(memory_space=SMEM)] + [vm] * 6,
        out_specs=[vm, vm],
        compiler_params=pltpu.CompilerParams(vmem_limit_bytes=16 * 2**20),
    )(at, inverse, amp, *parts)


def scatter_fit(parts):
    return [parts[0]] + [send(parts[s], fit_shift(s)) for s in (1, 2, 3)]


def gather_fit(own):
    return [own] + [send(own, fit_shift(-s)) for s in (1, 2, 3)]


def coupling_of(shard, at, margins, prepare, grant):
    half = SHARD // 2
    near_p = send(shard, ring(1, True))
    near_m = send(shard, ring(-1, True))
    far_p = send(near_p[:half], ring(1, True))
    far_m = send(near_m[half:], ring(-1, True))
    row = jnp.concatenate([shard, near_p, near_m, far_p, far_m])
    next_p = send(row, ring(1, False))
    next_m = send(row, ring(-1, False))
    row_x = send(row, SWAP)
    side = prepare()
    next_p, next_m, side = lax.optimization_barrier((next_p, next_m, side))
    half = ROW4 // 2
    last_p = send(next_p[:half], ring(1, False))
    last_m = send(next_m[half:], ring(-1, False))
    next_p_x = send(next_p, SWAP)
    next_m_x = send(next_m, SWAP)
    last_p_x = send(last_p, SWAP)
    last_m_x = send(last_m, SWAP)
    block = jnp.concatenate(
        [row, row_x, next_p, next_m, next_p_x, next_m_x, last_p, last_m, last_p_x, last_m_x]
    )
    two, one, three = products(False, at, side[0], side[1], margins, block, grant)
    sent = scatter_fit([None, one, two, three])[1:]
    own = products(True, at, side[0], side[1], margins, block, grant)
    return list(own) + sent, side


def shards(
    b_first,
    b_second,
    start_amplitudes,
    margins,
    fock_terms,
    partners,
    pno_energy,
    occ_energy,
    pair_list,
    pno_count,
):
    at = jnp.stack([lax.axis_index("pairs"), lax.axis_index("fit")]).astype(jnp.int32)
    packed = pack_start(at, pno_count, start_amplitudes)

    def prepare():
        where, *tables = make_tables(
            at, pair_list, pno_count, occ_energy, pno_energy, partners, start_amplitudes
        )
        ints = scatter_fit(integral_parts(at, b_first, b_second))
        return where, fock_terms, ints, tables

    cous, side = coupling_of(packed, at, margins, prepare, GRANTS[0])
    ints, (inverse, gap2, inverse2, keep2, start2) = side[2:]
    tables = (keep2, gap2, inverse2)
    rounded, prev = update(False, tables, start2, ints, cous)
    packed = jnp.concatenate(gather_fit(rounded))
    cous, _ = coupling_of(packed, at, margins, lambda: side, GRANTS[1])
    (res,) = update(True, tables, prev, ints, cous)
    amplitudes, residual = final(at, inverse, packed, gather_fit(res))
    return (amplitudes, residual)


def solution(mesh):
    return jax.shard_map(
        shards,
        mesh=mesh,
        in_specs=(
            P("pairs", None, "fit"),
            P("pairs", None, "fit"),
            P("pairs", None, None),
            P("pairs", "fit", None, None),
            P("pairs", "fit"),
            P("pairs", "fit"),
            P("pairs", None),
            P(),
            P("pairs", None),
            P("pairs"),
        ),
        out_specs=(P("pairs", None, None), P("pairs", None, None)),
        check_vma=False,
    )
```
